32 devices in a mesh: rep: 4 (over x, core), fsdp: 4 (over z), tp: 2 (over y).
Axes of the slice: x: 2, y: 2, z: 4, core: 2. Of those that a mesh axis runs over, the one named last changes fastest.
Arguments:
- inputs: bfloat16 [512, 4096], P('rep', 'tp'), may hold values from -6 to 6
- out_grads: bfloat16 [512, 14336], P('rep', 'fsdp'), may hold values from -0.5 to 0.5
- error: bfloat16 [4, 4096, 14336], P('rep', 'tp', 'fsdp'), may hold values from -20 to 20
- q_init: bfloat16 [14336, 64], P('fsdp'), may hold values from -6 to 6
Outputs:
- new_error: bfloat16 [4, 4096, 14336], P('rep', 'tp', 'fsdp')
- p_factor: bfloat16 [4096, 64], P('tp')
- q_factor: bfloat16 [14336, 64], P('fsdp')
The draws below stay inside these ranges and needn't reach their ends.
All inputs are finite; a program needn't handle non-finite values.
Results may differ from the reference program's by a relative error of at most 0.0014.
Values sent between devices are 32-bit elements; how exact they have to be, the bound alone decides.
A program may use at most 128 MiB of HBM per device.

```python
import math
import jax
import jax.numpy as jnp
from jax import lax

D = 4096
FF = 14336
R = 64
ITERS = 2
TOK = 128
REPLICAS = 4


def draw_error(key, part):
    key_noise = jax.random.fold_in(key, 11)
    key_rows = jax.random.fold_in(key, 12)
    key_cols = jax.random.fold_in(key, 13)
    row_pos = jnp.arange(D, dtype=jnp.float32) / max(D - 1, 1)
    row_scale = 3.0 ** row_pos * jnp.exp(jax.random.uniform(key_rows, (D,), jnp.float32, -0.4, 0.4))
    col_scale = jnp.exp(jax.random.uniform(key_cols, (FF,), jnp.float32, -0.7, 0.7))
    noise_draw = jax.random.truncated_normal(key_noise, -4.0, 4.0, (REPLICAS, D, FF), jnp.float32)
    scaled = 0.5 * noise_draw * row_scale[None, :, None] * col_scale[None, None, :]
    return scaled.astype(jnp.bfloat16)


def level_of(rng, shape, split, low, high):
    level = 1.0
    for axis_at, blocks in split:
        draws = jax.random.uniform(jax.random.fold_in(jax.random.fold_in(rng, 6), axis_at), (blocks,), jnp.float32, low / len(split), high / len(split))
        level = level * jnp.repeat(jnp.exp(draws), shape[axis_at] // blocks).reshape((-1,) + (1,) * (len(shape) - 1 - axis_at))
    return level


def scatter_about(stream_key, shape, deviation, limit, pieces=(), held_as=jnp.bfloat16):
    factor_of = level_of(stream_key, shape, pieces, -0.22, 0.18) if pieces else 1.0
    entries = jax.random.normal(stream_key, shape, jnp.float32) * deviation * factor_of
    return jnp.minimum(jnp.maximum(entries, -limit), limit).astype(held_as)


def setup_inputs(seed: int = 0) -> dict:
    streams_of = jax.random.split(jax.random.key(seed), 5)
    return {
        "inputs": scatter_about(streams_of[0], (REPLICAS * TOK, D), 1.0, 6.0, ((0, 4), (1, 2))),
        "out_grads": scatter_about(streams_of[1], (REPLICAS * TOK, FF), TOK ** -0.5, 0.5, ((0, 4), (1, 4))),
        "error": draw_error(jax.random.fold_in(streams_of[4], 71), 0),
        "q_init": scatter_about(streams_of[3], (FF, R), 1.0, 6.0, ((0, 4),)),
    }


exact_mode = lax.Precision.HIGHEST

def right_solve(factor, matrix):
    return jax.scipy.linalg.solve_triangular(factor, matrix.T, lower=True).T

def reference(inputs, out_grads, error, q_init):
    inputs_split = inputs.reshape(REPLICAS, TOK, D)
    grads_split = out_grads.reshape(REPLICAS, TOK, FF)

    def one_grad(pair):
        return lax.dot_general(pair[0].astype(jnp.float32), pair[1].astype(jnp.float32), (((0,), (0,)), ((), ())), preferred_element_type=jnp.float32)

    def accumulate(total, triple):
        merged = one_grad((triple[0], triple[1])) + triple[2].astype(jnp.float32)
        return (total + merged, None)
    summed, _ = lax.scan(accumulate, jnp.zeros((D, FF), jnp.float32), (inputs_split, grads_split, error))
    mean_merged = summed / REPLICAS
    q_full = q_init.astype(jnp.float32)
    p_basis = jnp.zeros((D, R), jnp.float32)
    for iteration in range(ITERS):
        p_full = jnp.dot(mean_merged, q_full, precision=exact_mode)
        gram = jnp.dot(p_full.T, p_full, precision=exact_mode)
        factor = jnp.linalg.cholesky(gram)
        p_basis = right_solve(factor, p_full)
        q_full = jnp.dot(mean_merged.T, p_basis, precision=exact_mode)
    approximation = jnp.dot(p_basis, q_full.T, precision=exact_mode)

    def new_one(triple):
        merged = one_grad((triple[0], triple[1])) + triple[2].astype(jnp.float32)
        return (merged - approximation).astype(jnp.bfloat16)
    new_error = lax.map(new_one, (inputs_split, grads_split, error))
    p_factor = (p_basis * math.sqrt(D)).astype(jnp.bfloat16)
    return (new_error, p_factor, q_full.astype(jnp.bfloat16))
```

```python
import functools
import math

import jax
import jax.numpy as jnp
from jax import lax
from jax.experimental import pallas as pl
from jax.experimental.pallas import tpu as pltpu
from jax.sharding import PartitionSpec as P

ITERS = 2
PIECES = 3
exact_mode = lax.Precision.HIGHEST
MESH = pl.DeviceIdType.MESH


def contract(left, right, at_left, at_right, precision=None):
    return lax.dot_general(
        left,
        right,
        (((at_left,), (at_right,)), ((), ())),
        precision=precision,
        preferred_element_type=jnp.float32,
    )


def pieces_of(value):
    pieces = []
    for _ in range(PIECES):
        piece = value.astype(jnp.bfloat16)
        pieces.append(piece)
        value = value - piece.astype(jnp.float32)
    return jnp.concatenate(pieces, axis=0)


def fold(stacked, rank):
    total = stacked[:rank]
    for at in range(rank, stacked.shape[0], rank):
        total = total + stacked[at : at + rank]
    return total


class Group:
    def __init__(self, axes, sizes):
        self.axes, self.sizes = axes, sizes
        self.count = sizes[0] * sizes[1]

    def me(self):
        return lax.axis_index(self.axes[0]) * self.sizes[1] + lax.axis_index(self.axes[1])

    def peer(self, step):
        at = lax.rem(self.me() + step, self.count)
        return at, {
            self.axes[0]: lax.div(at, self.sizes[1]),
            self.axes[1]: lax.rem(at, self.sizes[1]),
        }

    def meet(self):
        barrier = pltpu.get_barrier_semaphore()
        for step in range(1, self.count):
            pl.semaphore_signal(barrier, inc=1, device_id=self.peer(step)[1], device_id_type=MESH)
        pl.semaphore_wait(barrier, self.count - 1)

    def scatter(self, part_of, slots, send, recv):
        copies = []
        for step in range(1, self.count):
            at, device = self.peer(step)
            copies.append(
                pltpu.make_async_remote_copy(
                    part_of(at), slots.at[step - 1], send.at[step - 1], recv.at[step - 1],
                    device_id=device, device_id_type=MESH,
                )
            )
            copies[-1].start()
        return copies

    def share(self, part, send, recv):
        copies = []
        for step in range(1, self.count):
            _, device = self.peer(step)
            copies.append(
                pltpu.make_async_remote_copy(
                    part, part, send.at[step - 1], recv.at[step - 1],
                    device_id=device, device_id_type=MESH,
                )
            )
            copies[-1].start()
        return copies


def left_kernel(group, replicas, a_ref, q_ref, x_ref, g_ref, p_ref, p3_ref,
                total, slots, send, recv, send2, recv2):
    rank, columns = p_ref.shape
    width = columns // group.count
    inner = fold(contract(q_ref[...], g_ref[...], 1, 1), rank)
    outer = fold(contract(pieces_of(inner), x_ref[...], 1, 0), rank)
    total[...] = (outer + fold(a_ref[...], rank)) / replicas
    group.meet()

    def part(ref, at):
        return ref.at[:, pl.ds(pl.multiple_of(at * width, width), width)]

    copies = group.scatter(lambda at: part(total, at), slots, send, recv)
    mine = part(total, group.me())[...]
    for step, copy in enumerate(copies):
        copy.wait_recv()
        mine = mine + slots[step]
    part(p_ref, group.me())[...] = mine
    shared = group.share(part(p_ref, group.me()), send2, recv2)
    for copy in copies:
        copy.wait_send()
    for copy in shared:
        copy.wait()
    p3_ref[...] = pieces_of(p_ref[...])


def invert_into(grid, inverse):
    rank = grid.shape[0]
    lane = lax.broadcasted_iota(jnp.int32, grid.shape, 1)
    row_at = lax.broadcasted_iota(jnp.int32, (rank, 1), 0)

    def eliminate(j, carry):
        row = grid[pl.ds(j, 1), :]
        now = grid[...]
        column = jnp.sum(jnp.where(lane == rank + j, now, 0.0), axis=1, keepdims=True)
        pivot = jnp.sum(jnp.where(lane[:1] == rank + j, row, 0.0), axis=1, keepdims=True)
        inverse[pl.ds(j, 1), :] = row / jnp.sqrt(pivot)
        factor = jnp.where(row_at > j, column / pivot, 0.0)
        grid[...] = now - factor * row
        return carry

    lax.fori_loop(0, rank, eliminate, 0)


def right_kernel(group, pairs, replicas, a_ref, p_ref, p3_ref, x_ref, g_ref,
                 q_ref, q3_ref, basis_ref,
                 total, gathered, slots, mine_gram, gram_slots, grid, inverse,
                 send, recv, send2, recv2, gram_send, gram_recv):
    rank, columns = q_ref.shape
    height = rank // group.count
    inner = fold(contract(p3_ref[...], x_ref[...], 1, 1), rank)
    outer = fold(contract(pieces_of(inner), g_ref[...], 1, 0), rank)
    total[...] = (outer + fold(a_ref[...], rank)) / replicas
    left = p_ref[...]
    mine_gram[...] = contract(left, jnp.concatenate([left, left], axis=0), 1, 1, exact_mode)
    group.meet()

    def part(ref, at):
        return ref.at[pl.ds(pl.multiple_of(at * height, height), height), :]

    gram_copies = []
    for step in range(1, pairs):
        target = lax.rem(lax.axis_index("tp") + step, pairs)
        gram_copies.append(
            pltpu.make_async_remote_copy(
                mine_gram, gram_slots.at[step - 1], gram_send.at[step - 1], gram_recv.at[step - 1],
                device_id={"tp": target}, device_id_type=MESH,
            )
        )
        gram_copies[-1].start()
    copies = group.scatter(lambda at: part(total, at), slots, send, recv)
    gram = mine_gram[...]
    for step, copy in enumerate(gram_copies):
        copy.wait()
        gram = gram + gram_slots[step]
    lane = lax.broadcasted_iota(jnp.int32, gram.shape, 1)
    row_at = lax.broadcasted_iota(jnp.int32, gram.shape, 0)
    grid[...] = jnp.where(lane < rank, jnp.where(lane == row_at, 1.0, 0.0), gram)
    mine = part(total, group.me())[...]
    for step, copy in enumerate(copies):
        copy.wait_recv()
        mine = mine + slots[step]
    part(gathered, group.me())[...] = mine
    shared = group.share(part(gathered, group.me()), send2, recv2)
    invert_into(grid, inverse)
    for copy in copies:
        copy.wait_send()
    lower = inverse[:, :rank]
    basis_ref[...] = contract(lower, left, 1, 0, exact_mode)
    for copy in shared:
        copy.wait()
    result = contract(lower, gathered[...], 1, 0, exact_mode)
    q_ref[...] = result
    q3_ref[...] = pieces_of(result)


def vmem(count):
    return [pl.BlockSpec(memory_space=pltpu.VMEM)] * count


def dma(count):
    return pltpu.SemaphoreType.DMA((count,))


def left_call(tag, group, replicas, rank, a, q3, inputs, out_grads):
    columns = a.shape[1]
    width = columns // group.count
    others = group.count - 1
    return pl.pallas_call(
        functools.partial(left_kernel, group, replicas),
        name="left_reduce",
        out_shape=(
            jax.ShapeDtypeStruct((rank, columns), jnp.float32),
            jax.ShapeDtypeStruct((PIECES * rank, columns), jnp.bfloat16),
        ),
        in_specs=vmem(4),
        out_specs=vmem(2),
        scratch_shapes=[
            pltpu.VMEM((rank, columns), jnp.float32),
            pltpu.VMEM((others, rank, width), jnp.float32),
            dma(others), dma(others), dma(others), dma(others),
        ],
        compiler_params=pltpu.CompilerParams(collective_id=tag, has_side_effects=True, vmem_limit_bytes=40 << 20),
    )(a, q3, inputs, out_grads)


def right_call(group, pairs, replicas, rank, a, p, p3, inputs, out_grads):
    columns = a.shape[1]
    height = rank // group.count
    others = group.count - 1
    return pl.pallas_call(
        functools.partial(right_kernel, group, pairs, replicas),
        name="right_reduce",
        out_shape=(
            jax.ShapeDtypeStruct((rank, columns), jnp.float32),
            jax.ShapeDtypeStruct((PIECES * rank, columns), jnp.bfloat16),
            jax.ShapeDtypeStruct(p.shape, jnp.float32),
        ),
        in_specs=vmem(5),
        out_specs=vmem(3),
        scratch_shapes=[
            pltpu.VMEM((rank, columns), jnp.float32),
            pltpu.VMEM((rank, columns), jnp.float32),
            pltpu.VMEM((others, height, columns), jnp.float32),
            pltpu.VMEM((rank, 2 * rank), jnp.float32),
            pltpu.VMEM((pairs - 1, rank, 2 * rank), jnp.float32),
            pltpu.VMEM((rank, 2 * rank), jnp.float32),
            pltpu.VMEM((rank, 2 * rank), jnp.float32),
            dma(others), dma(others), dma(others), dma(others), dma(pairs - 1), dma(pairs - 1),
        ],
        compiler_params=pltpu.CompilerParams(collective_id=ITERS, has_side_effects=True, vmem_limit_bytes=40 << 20),
    )(a, p, p3, inputs, out_grads)


def rounded_pieces(value):
    pieces = []
    for _ in range(PIECES):
        piece = lax.reduce_precision(value, 8, 7)
        pieces.append(piece.astype(jnp.bfloat16))
        value = value - piece
    return jnp.concatenate(pieces, axis=0)


def plain_left(replicas, rank, a, q3, inputs, out_grads):
    inner = fold(contract(q3, out_grads, 1, 1), rank)
    outer = fold(contract(rounded_pieces(inner), inputs, 1, 0), rank)
    p = lax.psum((outer + fold(a, rank)) / replicas, ("rep", "fsdp"))
    return p, rounded_pieces(p)


def plain_right(replicas, rank, a, p, p3, inputs, out_grads):
    inner = fold(contract(p3, inputs, 1, 1), rank)
    outer = fold(contract(rounded_pieces(inner), out_grads, 1, 0), rank)
    q = lax.psum((outer + fold(a, rank)) / replicas, ("rep", "tp"))
    gram = lax.psum(contract(p, p, 1, 1, exact_mode), "tp")
    inverse = jax.scipy.linalg.solve_triangular(
        jnp.linalg.cholesky(gram), jnp.eye(rank, dtype=jnp.float32), lower=True
    )
    q = contract(inverse, q, 1, 0, exact_mode)
    return q, rounded_pieces(q), contract(inverse, p, 1, 0, exact_mode)


def shards(inputs, out_grads, error, q_init):
    replicas, splits, pairs = lax.axis_size("rep"), lax.axis_size("fsdp"), lax.axis_size("tp")
    rank = q_init.shape[1]
    rows, columns = error.shape[1:]
    left_group = Group(("rep", "fsdp"), (replicas, splits))
    right_group = Group(("rep", "tp"), (replicas, pairs))
    own_left = rows % (left_group.count * 128) == 0 and left_group.count > 1
    own_right = rank % (right_group.count * 8) == 0 and pairs > 1 and rank == 64
    error = error[0]
    q3 = q_init.T
    for iteration in range(ITERS):
        a = contract(q3, error, 1, 1)
        if own_left:
            p, p3 = left_call(iteration, left_group, replicas, rank, a, q3, inputs, out_grads)
        else:
            p, p3 = plain_left(replicas, rank, a, q3, inputs, out_grads)
        a = contract(p3, error, 1, 0)
        if own_right:
            q, q3, basis = right_call(right_group, pairs, replicas, rank, a, p, p3, inputs, out_grads)
        else:
            q, q3, basis = plain_right(replicas, rank, a, p, p3, inputs, out_grads)
    basis3 = rounded_pieces(-basis)
    high, low = basis3[:rank], basis3[rank : 2 * rank]
    lefts = jnp.concatenate([inputs, high, high, low], axis=0)
    rights = jnp.concatenate([out_grads, q3[:rank], q3[rank : 2 * rank], q3[:rank]], axis=0)
    merged = contract(lefts, rights, 0, 0) + error.astype(jnp.float32)
    p_factor = (basis * math.sqrt(rows * pairs)).astype(jnp.bfloat16).T
    return (merged.astype(jnp.bfloat16)[None], p_factor, q.astype(jnp.bfloat16).T)


def solution(mesh):
    in_specs = (P("rep", "tp"), P("rep", "fsdp"), P("rep", "tp", "fsdp"), P("fsdp", None))
    out_specs = (P("rep", "tp", "fsdp"), P("tp", None), P("fsdp", None))
    return jax.shard_map(shards, mesh=mesh, in_specs=in_specs, out_specs=out_specs, check_vma=False)
```

```python
import functools
import math

import jax
import jax.numpy as jnp
from jax import lax
from jax.experimental import pallas as pl
from jax.experimental.pallas import tpu as pltpu
from jax.sharding import PartitionSpec as P

ITERS = 2
PIECES = 3
BLOCK = 512
exact_mode = lax.Precision.HIGHEST
MESH = pl.DeviceIdType.MESH


def contract(left, right, at_left, at_right, precision=None):
    return lax.dot_general(
        left,
        right,
        (((at_left,), (at_right,)), ((), ())),
        precision=precision,
        preferred_element_type=jnp.float32,
    )


def pieces_of(value):
    pieces = []
    for _ in range(PIECES):
        piece = value.astype(jnp.bfloat16)
        pieces.append(piece)
        value = value - piece.astype(jnp.float32)
    return jnp.concatenate(pieces, axis=0)


def fold(stacked, rank):
    total = stacked[:rank]
    for at in range(rank, stacked.shape[0], rank):
        total = total + stacked[at : at + rank]
    return total


class Group:
    def __init__(self, axis, replicas, size):
        self.axis, self.size = axis, size
        self.count = (replicas // 2) * size

    def core(self):
        return lax.rem(lax.axis_index("rep"), 2)

    def me(self):
        return lax.div(lax.axis_index("rep"), 2) * self.size + lax.axis_index(self.axis)

    def at(self, step):
        return lax.rem(self.me() + step, self.count)

    def device(self, step):
        at = self.at(step)
        return {"rep": 2 * lax.div(at, self.size) + self.core(), self.axis: lax.rem(at, self.size)}

    def partner(self):
        return {"rep": lax.axis_index("rep") + 1 - 2 * self.core()}

    def greet(self):
        barrier = pltpu.get_barrier_semaphore()
        pl.semaphore_signal(barrier, inc=1, device_id=self.partner(), device_id_type=MESH)
        for step in range(1, self.count):
            pl.semaphore_signal(barrier, inc=1, device_id=self.device(step), device_id_type=MESH)

    def meet(self):
        pl.semaphore_wait(pltpu.get_barrier_semaphore(), self.count)


def push(source, target, sems, at, device):
    copy = pltpu.make_async_remote_copy(
        source, target, sems.at[0, at], sems.at[1, at], device_id=device, device_id_type=MESH
    )
    copy.start()
    return copy


def aligned(at, size):
    return pl.ds(pl.multiple_of(at * size, size), size)


def gather(group, part_of, share_sems, pass_sems):
    own = part_of(group.me())
    passed = [push(own, own, pass_sems, 0, group.partner())]
    shared = [
        push(own, own, share_sems, step - 1, group.device(step)) for step in range(1, group.count)
    ]

    def finish():
        for step in range(1, group.count):
            shared[step - 1].wait_recv()
            part = part_of(group.at(group.count - step))
            passed.append(push(part, part, pass_sems, step, group.partner()))
        for copy in shared:
            copy.wait_send()
        for copy in passed:
            copy.wait()

    return finish


def left_kernel(group, replicas, q_ref, x_ref, g_ref, e_ref, p_ref, p3_ref,
                held, total, outgoing, core_slots, slots,
                load_sems, core_sems, send_sems, share_sems, pass_sems):
    rank, columns = p_ref.shape
    count = group.count
    width, half = columns // count, rank // 2
    mine_rows, other_rows = aligned(group.core(), half), aligned(1 - group.core(), half)
    order = list(range(1, count)) + [0]
    loads = {}
    for step in order:
        rows = aligned(group.at(step), width)
        loads[step] = pltpu.make_async_copy(e_ref.at[0, rows, :], held.at[rows, :], load_sems.at[step])
        loads[step].start()
    group.greet()
    inner = fold(contract(q_ref[...], g_ref[...], 1, 1), rank)
    total[...] = fold(contract(pieces_of(inner), x_ref[...], 1, 0), rank)
    group.meet()
    core_copies, copies = {}, []

    def forward(step):
        core_copies[step].wait_recv()
        value = total[mine_rows, aligned(group.at(step), width)] + core_slots[step]
        if step == 0:
            return value
        outgoing[step - 1] = value
        copies.append(
            push(outgoing.at[step - 1], slots.at[step - 1], send_sems, step - 1, group.device(step))
        )

    for place, step in enumerate(order):
        span = aligned(group.at(step), width)
        loads[step].wait()
        product = fold(contract(q_ref[...], held[span, :], 1, 1), rank)
        total[:, span] = (total[:, span] + product) / replicas
        core_copies[step] = push(
            total.at[other_rows, span], core_slots.at[step], core_sems, step, group.partner()
        )
        if place:
            forward(order[place - 1])
    mine = forward(0)
    for step in range(1, count):
        copies[step - 1].wait_recv()
        mine = mine + slots[step - 1]
    p_ref[mine_rows, aligned(group.me(), width)] = mine
    finish = gather(
        group, lambda at: p_ref.at[mine_rows, aligned(at, width)], share_sems, pass_sems
    )
    for copy in copies:
        copy.wait_send()
    for step in order:
        core_copies[step].wait_send()
    finish()
    p3_ref[...] = pieces_of(p_ref[...])


def invert_into(grid, inverse):
    rank = grid.shape[0]
    lane = lax.broadcasted_iota(jnp.int32, grid.shape, 1)
    row_at = lax.broadcasted_iota(jnp.int32, (rank, 1), 0)

    def eliminate(j, carry):
        row = grid[pl.ds(j, 1), :]
        now = grid[...]
        column = jnp.sum(jnp.where(lane == rank + j, now, 0.0), axis=1, keepdims=True)
        pivot = jnp.sum(jnp.where(lane[:1] == rank + j, row, 0.0), axis=1, keepdims=True)
        inverse[pl.ds(j, 1), :] = row / jnp.sqrt(pivot)
        factor = jnp.where(row_at > j, column / pivot, 0.0)
        grid[...] = now - factor * row
        return carry

    lax.fori_loop(0, rank, eliminate, 0)


def right_kernel(group, pairs, replicas, p_ref, p3_ref, x_ref, g_ref, e_ref,
                 q_ref, q3_ref, basis_ref,
                 held, total, summed, gathered, core_slots, slots, own_gram, gram_slots, grid, inverse,
                 load_sems, core_sems, send_sems, share_sems, pass_sems, gram_sems):
    rank, columns = q_ref.shape
    count = group.count
    half, height = rank // 2, rank // 2 // count
    blocks, _, width = core_slots.shape
    mine_rows, other_rows = aligned(group.core(), half), aligned(1 - group.core(), half)
    loads = []
    for block in range(blocks):
        span = pl.ds(block * width, width)
        loads.append(
            pltpu.make_async_copy(e_ref.at[0, :, span], held.at[:, span], load_sems.at[block])
        )
        loads[-1].start()
    group.greet()
    inner = fold(contract(p3_ref[...], x_ref[...], 1, 1), rank)
    total[...] = fold(contract(pieces_of(inner), g_ref[...], 1, 0), rank)
    left = p_ref[...]
    own_gram[...] = contract(left, jnp.concatenate([left, left], axis=0), 1, 1, exact_mode)
    group.meet()
    gram_copies = []
    for step in range(1, pairs):
        target = lax.rem(lax.axis_index("tp") + step, pairs)
        gram_copies.append(
            push(own_gram, gram_slots.at[step - 1], gram_sems, step - 1, {"tp": target})
        )
    core_copies, copies = [], []

    def forward(block):
        span = pl.ds(block * width, width)
        core_copies[block].wait_recv()
        summed[:, span] = total[mine_rows, span] + core_slots[block]
        for step in range(1, count):
            copies.append(
                push(
                    summed.at[aligned(group.at(step), height), span],
                    slots.at[step - 1, :, span],
                    send_sems,
                    block * (count - 1) + step - 1,
                    group.device(step),
                )
            )

    for block in range(blocks):
        span = pl.ds(block * width, width)
        loads[block].wait()
        product = fold(contract(p3_ref[...], held[:, span], 1, 0), rank)
        total[:, span] = (total[:, span] + product) / replicas
        core_copies.append(
            push(total.at[other_rows, span], core_slots.at[block], core_sems, block, group.partner())
        )
        if block:
            forward(block - 1)
    forward(blocks - 1)
    gram = own_gram[...]
    for step, copy in enumerate(gram_copies):
        copy.wait()
        gram = gram + gram_slots[step]
    lane = lax.broadcasted_iota(jnp.int32, gram.shape, 1)
    row_at = lax.broadcasted_iota(jnp.int32, gram.shape, 0)
    grid[...] = jnp.where(lane < rank, jnp.where(lane == row_at, 1.0, 0.0), gram)

    def own_part(at):
        return gathered.at[aligned(group.core() * count + at, height), :]

    mine = summed[aligned(group.me(), height), :]
    for copy in copies:
        copy.wait_recv()
    for step in range(1, count):
        mine = mine + slots[step - 1]
    own_part(group.me())[...] = mine
    finish = gather(group, own_part, share_sems, pass_sems)
    invert_into(grid, inverse)
    lower = inverse[:, :rank]
    basis_ref[...] = contract(lower, left, 1, 0, exact_mode)
    for copy in copies + core_copies:
        copy.wait_send()
    finish()
    result = contract(lower, gathered[...], 1, 0, exact_mode)
    q_ref[...] = result
    q3_ref[...] = pieces_of(result)


def in_places():
    return [pl.BlockSpec(memory_space=pltpu.VMEM)] * 3 + [pl.BlockSpec(memory_space=pl.ANY)]


def dma(count):
    return pltpu.SemaphoreType.DMA((2, count))


def params(tag):
    return pltpu.CompilerParams(collective_id=tag, has_side_effects=True, vmem_limit_bytes=58 << 20)


def left_call(tag, group, replicas, rank, q3, inputs, out_grads, error):
    rows, columns = error.shape[1:]
    count, half = group.count, rank // 2
    width = rows // count
    return pl.pallas_call(
        functools.partial(left_kernel, group, replicas),
        name="left_reduce",
        out_shape=(
            jax.ShapeDtypeStruct((rank, rows), jnp.float32),
            jax.ShapeDtypeStruct((PIECES * rank, rows), jnp.bfloat16),
        ),
        in_specs=in_places(),
        out_specs=[pl.BlockSpec(memory_space=pltpu.VMEM)] * 2,
        scratch_shapes=[
            pltpu.VMEM((rows, columns), jnp.bfloat16),
            pltpu.VMEM((rank, rows), jnp.float32),
            pltpu.VMEM((count - 1, half, width), jnp.float32),
            pltpu.VMEM((count, half, width), jnp.float32),
            pltpu.VMEM((count - 1, half, width), jnp.float32),
            pltpu.SemaphoreType.DMA((count,)),
            dma(count), dma(count - 1), dma(count - 1), dma(count),
        ],
        compiler_params=params(tag),
    )(q3, inputs, out_grads, error)


def right_call(group, pairs, replicas, rank, p, p3, inputs, out_grads, error):
    rows, columns = error.shape[1:]
    count, half = group.count, rank // 2
    height, width = half // count, BLOCK
    blocks = columns // width
    others = count - 1
    return pl.pallas_call(
        functools.partial(right_kernel, group, pairs, replicas),
        name="right_reduce",
        out_shape=(
            jax.ShapeDtypeStruct((rank, columns), jnp.float32),
            jax.ShapeDtypeStruct((PIECES * rank, columns), jnp.bfloat16),
            jax.ShapeDtypeStruct(p.shape, jnp.float32),
        ),
        in_specs=[pl.BlockSpec(memory_space=pltpu.VMEM)] + in_places(),
        out_specs=[pl.BlockSpec(memory_space=pltpu.VMEM)] * 3,
        scratch_shapes=[
            pltpu.VMEM((rows, columns), jnp.bfloat16),
            pltpu.VMEM((rank, columns), jnp.float32),
            pltpu.VMEM((half, columns), jnp.float32),
            pltpu.VMEM((rank, columns), jnp.float32),
            pltpu.VMEM((blocks, half, width), jnp.float32),
            pltpu.VMEM((others, height, columns), jnp.float32),
            pltpu.VMEM((rank, 2 * rank), jnp.float32),
            pltpu.VMEM((pairs - 1, rank, 2 * rank), jnp.float32),
            pltpu.VMEM((rank, 2 * rank), jnp.float32),
            pltpu.VMEM((rank, 2 * rank), jnp.float32),
            pltpu.SemaphoreType.DMA((blocks,)),
            dma(blocks), dma(blocks * others), dma(others), dma(count), dma(pairs - 1),
        ],
        compiler_params=params(ITERS),
    )(p, p3, inputs, out_grads, error)


def rounded_pieces(value):
    pieces = []
    for _ in range(PIECES):
        piece = lax.reduce_precision(value, 8, 7)
        pieces.append(piece.astype(jnp.bfloat16))
        value = value - piece
    return jnp.concatenate(pieces, axis=0)


def plain_left(replicas, rank, a, q3, inputs, out_grads):
    inner = fold(contract(q3, out_grads, 1, 1), rank)
    outer = fold(contract(rounded_pieces(inner), inputs, 1, 0), rank)
    p = lax.psum((outer + fold(a, rank)) / replicas, ("rep", "fsdp"))
    return p, rounded_pieces(p)


def plain_right(replicas, rank, a, p, p3, inputs, out_grads):
    inner = fold(contract(p3, inputs, 1, 1), rank)
    outer = fold(contract(rounded_pieces(inner), out_grads, 1, 0), rank)
    q = lax.psum((outer + fold(a, rank)) / replicas, ("rep", "tp"))
    gram = lax.psum(contract(p, p, 1, 1, exact_mode), "tp")
    inverse = jax.scipy.linalg.solve_triangular(
        jnp.linalg.cholesky(gram), jnp.eye(rank, dtype=jnp.float32), lower=True
    )
    q = contract(inverse, q, 1, 0, exact_mode)
    return q, rounded_pieces(q), contract(inverse, p, 1, 0, exact_mode)


def shards(inputs, out_grads, error, q_init):
    replicas, splits, pairs = lax.axis_size("rep"), lax.axis_size("fsdp"), lax.axis_size("tp")
    rank = q_init.shape[1]
    rows, columns = error.shape[1:]
    left_group = Group("fsdp", replicas, splits)
    right_group = Group("tp", replicas, pairs)
    paired = replicas % 2 == 0 and rank == 64
    own_left = paired and left_group.count > 1 and rows % (left_group.count * 128) == 0
    own_right = (
        paired and pairs > 1 and rank % (right_group.count * 16) == 0 and columns % BLOCK == 0
    )
    q3 = q_init.T
    for iteration in range(ITERS):
        if own_left:
            p, p3 = left_call(iteration, left_group, replicas, rank, q3, inputs, out_grads, error)
        else:
            a = contract(q3, error[0], 1, 1)
            p, p3 = plain_left(replicas, rank, a, q3, inputs, out_grads)
        if own_right:
            q, q3, basis = right_call(
                right_group, pairs, replicas, rank, p, p3, inputs, out_grads, error
            )
        else:
            a = contract(p3, error[0], 1, 0)
            q, q3, basis = plain_right(replicas, rank, a, p, p3, inputs, out_grads)
    basis3 = rounded_pieces(-basis)
    high, low = basis3[:rank], basis3[rank : 2 * rank]
    lefts = jnp.concatenate([inputs, high, high, low], axis=0)
    rights = jnp.concatenate([out_grads, q3[:rank], q3[rank : 2 * rank], q3[:rank]], axis=0)
    merged = contract(lefts, rights, 0, 0) + error[0].astype(jnp.float32)
    p_factor = (basis * math.sqrt(rows * pairs)).astype(jnp.bfloat16).T
    return (merged.astype(jnp.bfloat16)[None], p_factor, q.astype(jnp.bfloat16).T)


def solution(mesh):
    in_specs = (P("rep", "tp"), P("rep", "fsdp"), P("rep", "tp", "fsdp"), P("fsdp", None))
    out_specs = (P("rep", "tp", "fsdp"), P("tp", None), P("fsdp", None))
    return jax.shard_map(shards, mesh=mesh, in_specs=in_specs, out_specs=out_specs, check_vma=False)
```

```python
import functools
import math

import jax
import jax.numpy as jnp
from jax import lax
from jax.experimental import pallas as pl
from jax.experimental.pallas import tpu as pltpu
from jax.sharding import PartitionSpec as P

ITERS = 2
PIECES = 3
BLOCK = 512
HEIGHT = 256
exact_mode = lax.Precision.HIGHEST
MESH = pl.DeviceIdType.MESH


def contract(left, right, at_left, at_right, precision=None):
    return lax.dot_general(
        left,
        right,
        (((at_left,), (at_right,)), ((), ())),
        precision=precision,
        preferred_element_type=jnp.float32,
    )


def pieces_of(value):
    pieces = []
    for _ in range(PIECES):
        piece = value.astype(jnp.bfloat16)
        pieces.append(piece)
        value = value - piece.astype(jnp.float32)
    return jnp.concatenate(pieces, axis=0)


def fold(stacked, rank):
    total = stacked[:rank]
    for at in range(rank, stacked.shape[0], rank):
        total = total + stacked[at : at + rank]
    return total


class Group:
    def __init__(self, axis, replicas, size):
        self.axis, self.size = axis, size
        self.count = (replicas // 2) * size
        self.wait_for = self.count

    def core(self):
        return lax.rem(lax.axis_index("rep"), 2)

    def me(self):
        return lax.div(lax.axis_index("rep"), 2) * self.size + lax.axis_index(self.axis)

    def at(self, step):
        return lax.rem(self.me() + step, self.count)

    def device(self, step):
        at = self.at(step)
        return {"rep": 2 * lax.div(at, self.size) + self.core(), self.axis: lax.rem(at, self.size)}

    def partner(self):
        return {"rep": lax.axis_index("rep") + 1 - 2 * self.core()}

    def greet(self):
        barrier = pltpu.get_barrier_semaphore()
        pl.semaphore_signal(barrier, inc=1, device_id=self.partner(), device_id_type=MESH)
        for step in range(1, self.count):
            pl.semaphore_signal(barrier, inc=1, device_id=self.device(step), device_id_type=MESH)

    def meet(self):
        pl.semaphore_wait(pltpu.get_barrier_semaphore(), self.wait_for)


def push(source, target, sems, at, device):
    copy = pltpu.make_async_remote_copy(
        source, target, sems.at[0, at], sems.at[1, at], device_id=device, device_id_type=MESH
    )
    copy.start()
    return copy


def aligned(at, size):
    return pl.ds(pl.multiple_of(at * size, size), size)


def gather(group, part_of, share_sems, pass_sems):
    own = part_of(group.me())
    passed = [push(own, own, pass_sems, 0, group.partner())]
    shared = [
        push(own, own, share_sems, step - 1, group.device(step)) for step in range(1, group.count)
    ]

    def finish():
        for step in range(1, group.count):
            shared[step - 1].wait_recv()
            part = part_of(group.at(group.count - step))
            passed.append(push(part, part, pass_sems, step, group.partner()))
        for copy in shared:
            copy.wait_send()
        for copy in passed:
            copy.wait()

    return finish


def left_phase(group, replicas, loads, q_ref, x_ref, g_ref, p3_ref, held,
               p_ref, total, outgoing, core_slots, slots,
               core_sems, send_sems, share_sems, pass_sems):
    rank, columns = p_ref.shape
    count = group.count
    width, half = columns // count, rank // 2
    mine_rows, other_rows = aligned(group.core(), half), aligned(1 - group.core(), half)
    order = list(range(1, count)) + [0]
    inner = fold(contract(q_ref[...], g_ref[...], 1, 1), rank)
    total[...] = fold(contract(pieces_of(inner), x_ref[...], 1, 0), rank)
    if loads is not None:
        group.meet()
    core_copies, copies = {}, []

    def forward(step):
        core_copies[step].wait_recv()
        value = total[mine_rows, aligned(group.at(step), width)] + core_slots[step]
        if step == 0:
            return value
        outgoing[step - 1] = value
        copies.append(
            push(outgoing.at[step - 1], slots.at[step - 1], send_sems, step - 1, group.device(step))
        )

    for place, step in enumerate(order):
        span = aligned(group.at(step), width)
        if loads is not None:
            loads[step].wait()
        product = fold(contract(q_ref[...], held[span, :], 1, 1), rank)
        total[:, span] = (total[:, span] + product) / replicas
        core_copies[step] = push(
            total.at[other_rows, span], core_slots.at[step], core_sems, step, group.partner()
        )
        if place:
            forward(order[place - 1])
    mine = forward(0)
    for step in range(1, count):
        copies[step - 1].wait_recv()
        mine = mine + slots[step - 1]
    p_ref[mine_rows, aligned(group.me(), width)] = mine
    finish = gather(
        group, lambda at: p_ref.at[mine_rows, aligned(at, width)], share_sems, pass_sems
    )
    for copy in copies:
        copy.wait_send()
    for step in order:
        core_copies[step].wait_send()
    finish()
    p3_ref[...] = pieces_of(p_ref[...])


def invert_into(grid, inverse):
    rank = grid.shape[0]
    lane = lax.broadcasted_iota(jnp.int32, grid.shape, 1)
    row_at = lax.broadcasted_iota(jnp.int32, (rank, 1), 0)

    def eliminate(j, carry):
        row = grid[pl.ds(j, 1), :]
        now = grid[...]
        column = jnp.sum(jnp.where(lane == rank + j, now, 0.0), axis=1, keepdims=True)
        pivot = jnp.sum(jnp.where(lane[:1] == rank + j, row, 0.0), axis=1, keepdims=True)
        inverse[pl.ds(j, 1), :] = row / jnp.sqrt(pivot)
        factor = jnp.where(row_at > j, column / pivot, 0.0)
        grid[...] = now - factor * row
        return carry

    lax.fori_loop(0, rank, eliminate, 0)


def right_phase(group, pairs, replicas, p_ref, p3_ref, x_ref, g_ref, q3_ref, basis_ref, held,
                total, summed, gathered, core_slots, slots, own_gram, gram_slots, grid, inverse,
                core_sems, send_sems, share_sems, pass_sems, gram_sems):
    rank, columns = total.shape
    count = group.count
    half, height = rank // 2, rank // 2 // count
    blocks, _, width = core_slots.shape
    mine_rows, other_rows = aligned(group.core(), half), aligned(1 - group.core(), half)
    inner = fold(contract(p3_ref[...], x_ref[...], 1, 1), rank)
    total[...] = fold(contract(pieces_of(inner), g_ref[...], 1, 0), rank)
    left = p_ref[...]
    own_gram[...] = contract(left, jnp.concatenate([left, left], axis=0), 1, 1, exact_mode)
    gram_copies = []
    for step in range(1, pairs):
        target = lax.rem(lax.axis_index("tp") + step, pairs)
        gram_copies.append(
            push(own_gram, gram_slots.at[step - 1], gram_sems, step - 1, {"tp": target})
        )
    core_copies, copies = [], []

    def forward(block):
        span = pl.ds(block * width, width)
        core_copies[block].wait_recv()
        summed[:, span] = total[mine_rows, span] + core_slots[block]
        for step in range(1, count):
            copies.append(
                push(
                    summed.at[aligned(group.at(step), height), span],
                    slots.at[step - 1, :, span],
                    send_sems,
                    block * (count - 1) + step - 1,
                    group.device(step),
                )
            )

    for block in range(blocks):
        span = pl.ds(block * width, width)
        product = fold(contract(p3_ref[...], held[:, span], 1, 0), rank)
        total[:, span] = (total[:, span] + product) / replicas
        core_copies.append(
            push(total.at[other_rows, span], core_slots.at[block], core_sems, block, group.partner())
        )
        if block:
            forward(block - 1)
    forward(blocks - 1)
    gram = own_gram[...]
    for step, copy in enumerate(gram_copies):
        copy.wait()
        gram = gram + gram_slots[step]
    lane = lax.broadcasted_iota(jnp.int32, gram.shape, 1)
    row_at = lax.broadcasted_iota(jnp.int32, gram.shape, 0)
    grid[...] = jnp.where(lane < rank, jnp.where(lane == row_at, 1.0, 0.0), gram)

    def own_part(at):
        return gathered.at[aligned(group.core() * count + at, height), :]

    mine = summed[aligned(group.me(), height), :]
    for copy in copies:
        copy.wait_recv()
    for step in range(1, count):
        mine = mine + slots[step - 1]
    own_part(group.me())[...] = mine
    finish = gather(group, own_part, share_sems, pass_sems)
    invert_into(grid, inverse)
    lower = inverse[:, :rank]
    if basis_ref is not None:
        basis_ref[...] = contract(lower, left, 1, 0, exact_mode)
    for copy in copies + core_copies:
        copy.wait_send()
    finish()
    q3_ref[...] = pieces_of(contract(lower, gathered[...], 1, 0, exact_mode))


LEFT_REFS, RIGHT_REFS = 9, 14


def factor_kernel(left_group, right_group, pairs, replicas, q_ref, x_ref, g_ref, e_ref,
                  q3_ref, basis_ref, held, p3_ref, load_sems, *refs):
    columns = held.shape[0]
    count = left_group.count
    width = columns // count
    loads = {}
    for step in list(range(1, count)) + [0]:
        rows = aligned(left_group.at(step), width)
        loads[step] = pltpu.make_async_copy(e_ref.at[0, rows, :], held.at[rows, :], load_sems.at[step])
        loads[step].start()
    barrier = pltpu.get_barrier_semaphore()
    left_group.greet()
    for step in range(1, right_group.count):
        pl.semaphore_signal(barrier, inc=1, device_id=right_group.device(step), device_id_type=MESH)
    left_group.wait_for = left_group.count + right_group.count - 1
    for iteration in range(ITERS):
        left, refs = refs[:LEFT_REFS], refs[LEFT_REFS:]
        right, refs = refs[:RIGHT_REFS], refs[RIGHT_REFS:]
        left_phase(
            left_group, replicas, None if iteration else loads,
            q3_ref if iteration else q_ref, x_ref, g_ref, p3_ref, held, *left,
        )
        right_phase(
            right_group, pairs, replicas, left[0], p3_ref, x_ref, g_ref, q3_ref,
            basis_ref if iteration == ITERS - 1 else None, held, *right,
        )


def dma(count):
    return pltpu.SemaphoreType.DMA((2, count))


def f32(*shape):
    return pltpu.VMEM(shape, jnp.float32)


def factor_call(left_group, right_group, pairs, replicas, rank, q3, inputs, out_grads, error):
    rows, columns = error.shape[1:]
    half = rank // 2
    n, m = left_group.count, right_group.count
    width, height, blocks = rows // n, half // m, columns // BLOCK
    left = [
        f32(rank, rows), f32(rank, rows), f32(n - 1, half, width), f32(n, half, width),
        f32(n - 1, half, width), dma(n), dma(n - 1), dma(n - 1), dma(n),
    ]
    square = (rank, 2 * rank)
    right = [
        f32(rank, columns), f32(half, columns), f32(rank, columns), f32(blocks, half, BLOCK),
        f32(m - 1, height, columns), f32(*square), f32(pairs - 1, *square), f32(*square),
        f32(*square), dma(blocks), dma(blocks * (m - 1)), dma(m - 1), dma(m), dma(pairs - 1),
    ]
    vmem = pl.BlockSpec(memory_space=pltpu.VMEM)
    return pl.pallas_call(
        functools.partial(factor_kernel, left_group, right_group, pairs, replicas),
        name="factors",
        out_shape=(
            jax.ShapeDtypeStruct((PIECES * rank, columns), jnp.bfloat16),
            jax.ShapeDtypeStruct((rank, rows), jnp.float32),
        ),
        in_specs=[vmem, vmem, vmem, pl.BlockSpec(memory_space=pl.ANY)],
        out_specs=[vmem, vmem],
        scratch_shapes=[
            pltpu.VMEM((rows, columns), jnp.bfloat16),
            pltpu.VMEM((PIECES * rank, rows), jnp.bfloat16),
            pltpu.SemaphoreType.DMA((n,)),
        ]
        + (left + right) * ITERS,
        compiler_params=pltpu.CompilerParams(
            collective_id=0, has_side_effects=True, vmem_limit_bytes=58 << 20
        ),
    )(q3, inputs, out_grads, error)


def residual_kernel(scale, x_ref, g_ref, q3_ref, basis_ref, e_ref,
                    error_ref, p_ref, q_ref, lefts, rights):
    rank = basis_ref.shape[0]
    height, columns = e_ref.shape[1:]
    step = pl.program_id(0)

    @pl.when(step == 0)
    def _():
        basis = basis_ref[...]
        pieces = pieces_of(-basis)
        high, low = pieces[:rank], pieces[rank : 2 * rank]
        lefts[...] = jnp.concatenate([x_ref[...], high, high, low], axis=0)
        q_high, q_low = q3_ref[:rank], q3_ref[rank : 2 * rank]
        rights[...] = jnp.concatenate([g_ref[...], q_high, q_low, q_high], axis=0)
        p_ref[...] = (basis * scale).astype(jnp.bfloat16)
        q_ref[...] = q_high

    left = lefts[:, aligned(step, height)].T
    for at in range(0, columns, BLOCK):
        span = pl.ds(at, BLOCK)
        merged = contract(left, rights[:, span], 1, 0) + e_ref[0, :, span].astype(jnp.float32)
        error_ref[0, :, span] = merged.astype(jnp.bfloat16)


def residual_call(pairs, q3, basis, inputs, out_grads, error):
    rank = basis.shape[0]
    rows, columns = error.shape[1:]
    depth = inputs.shape[0] + 3 * rank
    height = HEIGHT

    def fixed(shape):
        return pl.BlockSpec(shape, lambda step: (0, 0))

    block = pl.BlockSpec((1, height, columns), lambda step: (0, step, 0))
    return pl.pallas_call(
        functools.partial(residual_kernel, math.sqrt(rows * pairs)),
        name="residual",
        grid=(rows // height,),
        out_shape=(
            jax.ShapeDtypeStruct(error.shape, jnp.bfloat16),
            jax.ShapeDtypeStruct((rank, rows), jnp.bfloat16),
            jax.ShapeDtypeStruct((rank, columns), jnp.bfloat16),
        ),
        in_specs=[fixed(v.shape) for v in (inputs, out_grads, q3, basis)] + [block],
        out_specs=[block, fixed((rank, rows)), fixed((rank, columns))],
        scratch_shapes=[
            pltpu.VMEM((depth, rows), jnp.bfloat16),
            pltpu.VMEM((depth, columns), jnp.bfloat16),
        ],
        compiler_params=pltpu.CompilerParams(vmem_limit_bytes=40 << 20),
    )(inputs, out_grads, q3, basis, error)


def rounded_pieces(value):
    pieces = []
    for _ in range(PIECES):
        piece = lax.reduce_precision(value, 8, 7)
        pieces.append(piece.astype(jnp.bfloat16))
        value = value - piece
    return jnp.concatenate(pieces, axis=0)


def plain_left(replicas, rank, a, q3, inputs, out_grads):
    inner = fold(contract(q3, out_grads, 1, 1), rank)
    outer = fold(contract(rounded_pieces(inner), inputs, 1, 0), rank)
    p = lax.psum((outer + fold(a, rank)) / replicas, ("rep", "fsdp"))
    return p, rounded_pieces(p)


def plain_right(replicas, rank, a, p, p3, inputs, out_grads):
    inner = fold(contract(p3, inputs, 1, 1), rank)
    outer = fold(contract(rounded_pieces(inner), out_grads, 1, 0), rank)
    q = lax.psum((outer + fold(a, rank)) / replicas, ("rep", "tp"))
    gram = lax.psum(contract(p, p, 1, 1, exact_mode), "tp")
    inverse = jax.scipy.linalg.solve_triangular(
        jnp.linalg.cholesky(gram), jnp.eye(rank, dtype=jnp.float32), lower=True
    )
    q = contract(inverse, q, 1, 0, exact_mode)
    return q, rounded_pieces(q), contract(inverse, p, 1, 0, exact_mode)


def shards(inputs, out_grads, error, q_init):
    replicas, splits, pairs = lax.axis_size("rep"), lax.axis_size("fsdp"), lax.axis_size("tp")
    rank = q_init.shape[1]
    rows, columns = error.shape[1:]
    left_group = Group("fsdp", replicas, splits)
    right_group = Group("tp", replicas, pairs)
    if (
        replicas % 2 == 0 and rank == 64 and pairs > 1 and left_group.count > 1
        and rows % (left_group.count * 128) == 0 and rows % HEIGHT == 0
        and rank % (right_group.count * 16) == 0 and columns % BLOCK == 0
    ):
        q3, basis = factor_call(
            left_group, right_group, pairs, replicas, rank, q_init.T, inputs, out_grads, error
        )
        new_error, p_factor, q_factor = residual_call(
            pairs, q3, basis, inputs, out_grads, error
        )
        return (new_error, p_factor.T, q_factor.T)
    q3 = q_init.T
    for _ in range(ITERS):
        a = contract(q3, error[0], 1, 1)
        p, p3 = plain_left(replicas, rank, a, q3, inputs, out_grads)
        a = contract(p3, error[0], 1, 0)
        q, q3, basis = plain_right(replicas, rank, a, p, p3, inputs, out_grads)
    basis3 = rounded_pieces(-basis)
    high, low = basis3[:rank], basis3[rank : 2 * rank]
    lefts = jnp.concatenate([inputs, high, high, low], axis=0)
    rights = jnp.concatenate([out_grads, q3[:rank], q3[rank : 2 * rank], q3[:rank]], axis=0)
    merged = contract(lefts, rights, 0, 0) + error[0].astype(jnp.float32)
    p_factor = (basis * math.sqrt(rows * pairs)).astype(jnp.bfloat16).T
    return (merged.astype(jnp.bfloat16)[None], p_factor, q.astype(jnp.bfloat16).T)


def solution(mesh):
    in_specs = (P("rep", "tp"), P("rep", "fsdp"), P("rep", "tp", "fsdp"), P("fsdp", None))
    out_specs = (P("rep", "tp", "fsdp"), P("tp", None), P("fsdp", None))
    return jax.shard_map(shards, mesh=mesh, in_specs=in_specs, out_specs=out_specs, check_vma=False)
```

```python
import functools
import math

import jax
import jax.numpy as jnp
from jax import lax
from jax.experimental import pallas as pl
from jax.experimental.pallas import tpu as pltpu
from jax.sharding import PartitionSpec as P

ITERS = 2
PIECES = 3
BLOCK = 512
HEIGHT = 512
exact_mode = lax.Precision.HIGHEST
MESH = pl.DeviceIdType.MESH


def contract(left, right, at_left, at_right, precision=None):
    return lax.dot_general(
        left,
        right,
        (((at_left,), (at_right,)), ((), ())),
        precision=precision,
        preferred_element_type=jnp.float32,
    )


def pieces_of(value):
    pieces = []
    for _ in range(PIECES):
        piece = value.astype(jnp.bfloat16)
        pieces.append(piece)
        value = value - piece.astype(jnp.float32)
    return jnp.concatenate(pieces, axis=0)


def full_product(left, right):
    turned, split = pieces_of(left.T), pieces_of(right)
    rank = left.shape[1]
    pairs = [(0, 0), (0, 1), (1, 0), (0, 2), (2, 0), (1, 1)]
    lefts = [turned[a * rank : (a + 1) * rank] for a, _ in pairs]
    rights = [split[b * rank : (b + 1) * rank] for _, b in pairs]
    return contract(jnp.concatenate(lefts, axis=0), jnp.concatenate(rights, axis=0), 0, 0)


def fold(stacked, rank):
    total = stacked[:rank]
    for at in range(rank, stacked.shape[0], rank):
        total = total + stacked[at : at + rank]
    return total


class Group:
    def __init__(self, axis, replicas, size):
        self.axis, self.size = axis, size
        self.count = (replicas // 2) * size
        self.wait_for = self.count

    def core(self):
        return lax.rem(lax.axis_index("rep"), 2)

    def me(self):
        return lax.div(lax.axis_index("rep"), 2) * self.size + lax.axis_index(self.axis)

    def at(self, step):
        return lax.rem(self.me() + step, self.count)

    def device(self, step):
        at = self.at(step)
        return {"rep": 2 * lax.div(at, self.size) + self.core(), self.axis: lax.rem(at, self.size)}

    def partner(self):
        return {"rep": lax.axis_index("rep") + 1 - 2 * self.core()}

    def greet(self):
        barrier = pltpu.get_barrier_semaphore()
        pl.semaphore_signal(barrier, inc=1, device_id=self.partner(), device_id_type=MESH)
        for step in range(1, self.count):
            pl.semaphore_signal(barrier, inc=1, device_id=self.device(step), device_id_type=MESH)

    def meet(self):
        pl.semaphore_wait(pltpu.get_barrier_semaphore(), self.wait_for)


def push(source, target, sems, at, device):
    copy = pltpu.make_async_remote_copy(
        source, target, sems.at[0, at], sems.at[1, at], device_id=device, device_id_type=MESH
    )
    copy.start()
    return copy


def aligned(at, size):
    return pl.ds(pl.multiple_of(at * size, size), size)


def gather(group, part_of, share_sems, pass_sems):
    own = part_of(group.me())
    passed = [push(own, own, pass_sems, 0, group.partner())]
    shared = [
        push(own, own, share_sems, step - 1, group.device(step)) for step in range(1, group.count)
    ]

    def finish():
        for step in range(1, group.count):
            shared[step - 1].wait_recv()
            part = part_of(group.at(group.count - step))
            passed.append(push(part, part, pass_sems, step, group.partner()))
        for copy in shared:
            copy.wait_send()
        for copy in passed:
            copy.wait()

    return finish


def left_phase(group, replicas, loads, q_ref, x_ref, g_ref, p3_ref, held,
               p_ref, total, outgoing, core_slots, slots,
               core_sems, send_sems, share_sems, pass_sems):
    rank, columns = p_ref.shape
    count = group.count
    width, half = columns // count, rank // 2
    mine_rows, other_rows = aligned(group.core(), half), aligned(1 - group.core(), half)
    order = list(range(1, count)) + [0]
    inner = fold(contract(q_ref[...], g_ref[...], 1, 1), rank)
    total[...] = fold(contract(pieces_of(inner), x_ref[...], 1, 0), rank)
    if loads is not None:
        group.meet()
    core_copies, copies = {}, []

    def forward(step):
        core_copies[step].wait_recv()
        value = total[mine_rows, aligned(group.at(step), width)] + core_slots[step]
        if step == 0:
            return value
        outgoing[step - 1] = value
        copies.append(
            push(outgoing.at[step - 1], slots.at[step - 1], send_sems, step - 1, group.device(step))
        )

    for place, step in enumerate(order):
        span = aligned(group.at(step), width)
        if loads is not None:
            loads[step].wait()
        product = fold(contract(q_ref[...], held[span, :], 1, 1), rank)
        total[:, span] = (total[:, span] + product) / replicas
        core_copies[step] = push(
            total.at[other_rows, span], core_slots.at[step], core_sems, step, group.partner()
        )
        if place:
            forward(order[place - 1])
    mine = forward(0)
    for step in range(1, count):
        copies[step - 1].wait_recv()
        mine = mine + slots[step - 1]
    p_ref[mine_rows, aligned(group.me(), width)] = mine
    finish = gather(
        group, lambda at: p_ref.at[mine_rows, aligned(at, width)], share_sems, pass_sems
    )
    for copy in copies:
        copy.wait_send()
    for step in order:
        core_copies[step].wait_send()
    finish()
    p3_ref[...] = pieces_of(p_ref[...])


def invert_into(grid, inverse):
    rank = grid.shape[0]
    lane = lax.broadcasted_iota(jnp.int32, grid.shape, 1)
    row_at = lax.broadcasted_iota(jnp.int32, (rank, 1), 0)

    def eliminate(j, carry):
        row = grid[pl.ds(j, 1), :]
        now = grid[...]
        column = jnp.sum(jnp.where(lane == rank + j, now, 0.0), axis=1, keepdims=True)
        pivot = jnp.sum(jnp.where(lane[:1] == rank + j, row, 0.0), axis=1, keepdims=True)
        inverse[pl.ds(j, 1), :] = row / jnp.sqrt(pivot)
        factor = jnp.where(row_at > j, column / pivot, 0.0)
        grid[...] = now - factor * row
        return carry

    lax.fori_loop(0, rank, eliminate, 0)


def right_phase(group, pairs, replicas, p_ref, p3_ref, x_ref, g_ref, q3_ref, basis_ref, held,
                total, summed, gathered, core_slots, slots, own_gram, gram_slots, grid, inverse,
                core_sems, send_sems, share_sems, pass_sems, gram_sems):
    rank, columns = total.shape
    count = group.count
    half, height = rank // 2, rank // 2 // count
    blocks, _, width = core_slots.shape
    mine_rows, other_rows = aligned(group.core(), half), aligned(1 - group.core(), half)
    inner = fold(contract(p3_ref[...], x_ref[...], 1, 1), rank)
    total[...] = fold(contract(pieces_of(inner), g_ref[...], 1, 0), rank)
    left = p_ref[...]
    own_gram[...] = contract(left, jnp.concatenate([left, left], axis=0), 1, 1, exact_mode)
    gram_copies = []
    for step in range(1, pairs):
        target = lax.rem(lax.axis_index("tp") + step, pairs)
        gram_copies.append(
            push(own_gram, gram_slots.at[step - 1], gram_sems, step - 1, {"tp": target})
        )
    core_copies, copies = [], []

    def forward(block):
        span = pl.ds(block * width, width)
        core_copies[block].wait_recv()
        summed[:, span] = total[mine_rows, span] + core_slots[block]
        for step in range(1, count):
            copies.append(
                push(
                    summed.at[aligned(group.at(step), height), span],
                    slots.at[step - 1, :, span],
                    send_sems,
                    block * (count - 1) + step - 1,
                    group.device(step),
                )
            )

    for block in range(blocks):
        span = pl.ds(block * width, width)
        product = fold(contract(p3_ref[...], held[:, span], 1, 0), rank)
        total[:, span] = (total[:, span] + product) / replicas
        core_copies.append(
            push(total.at[other_rows, span], core_slots.at[block], core_sems, block, group.partner())
        )
        if block:
            forward(block - 1)
    forward(blocks - 1)
    gram = own_gram[...]
    for step, copy in enumerate(gram_copies):
        copy.wait()
        gram = gram + gram_slots[step]
    lane = lax.broadcasted_iota(jnp.int32, gram.shape, 1)
    row_at = lax.broadcasted_iota(jnp.int32, gram.shape, 0)
    grid[...] = jnp.where(lane < rank, jnp.where(lane == row_at, 1.0, 0.0), gram)

    def own_part(at):
        return gathered.at[aligned(group.core() * count + at, height), :]

    mine = summed[aligned(group.me(), height), :]
    for copy in copies:
        copy.wait_recv()
    for step in range(1, count):
        mine = mine + slots[step - 1]
    own_part(group.me())[...] = mine
    finish = gather(group, own_part, share_sems, pass_sems)
    invert_into(grid, inverse)
    lower = inverse[:, :rank]
    if basis_ref is not None:
        basis_ref[...] = full_product(lower, left)
    for copy in copies + core_copies:
        copy.wait_send()
    finish()
    q3_ref[...] = pieces_of(full_product(lower, gathered[...]))


LEFT_REFS, RIGHT_REFS = 9, 14


def factor_kernel(left_group, right_group, pairs, replicas, q_ref, x_ref, g_ref, e_ref,
                  q3_ref, basis_ref, held, p3_ref, load_sems, *refs):
    columns = held.shape[0]
    count = left_group.count
    width = columns // count
    loads = {}
    for step in list(range(1, count)) + [0]:
        rows = aligned(left_group.at(step), width)
        loads[step] = pltpu.make_async_copy(e_ref.at[0, rows, :], held.at[rows, :], load_sems.at[step])
        loads[step].start()
    barrier = pltpu.get_barrier_semaphore()
    left_group.greet()
    for step in range(1, right_group.count):
        pl.semaphore_signal(barrier, inc=1, device_id=right_group.device(step), device_id_type=MESH)
    left_group.wait_for = left_group.count + right_group.count - 1
    for iteration in range(ITERS):
        left, refs = refs[:LEFT_REFS], refs[LEFT_REFS:]
        right, refs = refs[:RIGHT_REFS], refs[RIGHT_REFS:]
        left_phase(
            left_group, replicas, None if iteration else loads,
            q3_ref if iteration else q_ref, x_ref, g_ref, p3_ref, held, *left,
        )
        right_phase(
            right_group, pairs, replicas, left[0], p3_ref, x_ref, g_ref, q3_ref,
            basis_ref if iteration == ITERS - 1 else None, held, *right,
        )


def dma(count):
    return pltpu.SemaphoreType.DMA((2, count))


def f32(*shape):
    return pltpu.VMEM(shape, jnp.float32)


def factor_call(left_group, right_group, pairs, replicas, rank, q3, inputs, out_grads, error):
    rows, columns = error.shape[1:]
    half = rank // 2
    n, m = left_group.count, right_group.count
    width, height, blocks = rows // n, half // m, columns // BLOCK
    left = [
        f32(rank, rows), f32(rank, rows), f32(n - 1, half, width), f32(n, half, width),
        f32(n - 1, half, width), dma(n), dma(n - 1), dma(n - 1), dma(n),
    ]
    square = (rank, 2 * rank)
    right = [
        f32(rank, columns), f32(half, columns), f32(rank, columns), f32(blocks, half, BLOCK),
        f32(m - 1, height, columns), f32(*square), f32(pairs - 1, *square), f32(*square),
        f32(*square), dma(blocks), dma(blocks * (m - 1)), dma(m - 1), dma(m), dma(pairs - 1),
    ]
    vmem = pl.BlockSpec(memory_space=pltpu.VMEM)
    return pl.pallas_call(
        functools.partial(factor_kernel, left_group, right_group, pairs, replicas),
        name="factors",
        out_shape=(
            jax.ShapeDtypeStruct((PIECES * rank, columns), jnp.bfloat16),
            jax.ShapeDtypeStruct((rank, rows), jnp.float32),
        ),
        in_specs=[vmem, vmem, vmem, pl.BlockSpec(memory_space=pl.ANY)],
        out_specs=[vmem, vmem],
        scratch_shapes=[
            pltpu.VMEM((rows, columns), jnp.bfloat16),
            pltpu.VMEM((PIECES * rank, rows), jnp.bfloat16),
            pltpu.SemaphoreType.DMA((n,)),
        ]
        + (left + right) * ITERS,
        compiler_params=pltpu.CompilerParams(
            collective_id=0, has_side_effects=True, vmem_limit_bytes=50 << 20
        ),
    )(q3, inputs, out_grads, error)


def residual_kernel(scale, x_ref, g_ref, q3_ref, basis_ref, e_ref,
                    error_ref, p_ref, q_ref, lefts, rights):
    rank = basis_ref.shape[0]
    height, columns = e_ref.shape[1:]
    step = pl.program_id(0)

    @pl.when(step == 0)
    def _():
        basis = basis_ref[...]
        pieces = pieces_of(-basis)
        high, low = pieces[:rank], pieces[rank : 2 * rank]
        lefts[...] = jnp.concatenate([x_ref[...], high, high, low], axis=0)
        q_high, q_low = q3_ref[:rank], q3_ref[rank : 2 * rank]
        rights[...] = jnp.concatenate([g_ref[...], q_high, q_low, q_high], axis=0)
        p_ref[...] = (basis * scale).astype(jnp.bfloat16)
        q_ref[...] = q_high

    left = lefts[:, aligned(step, height)].T
    for at in range(0, columns, BLOCK):
        span = pl.ds(at, BLOCK)
        merged = contract(left, rights[:, span], 1, 0) + e_ref[0, :, span].astype(jnp.float32)
        error_ref[0, :, span] = merged.astype(jnp.bfloat16)


def residual_call(pairs, q3, basis, inputs, out_grads, error):
    rank = basis.shape[0]
    rows, columns = error.shape[1:]
    depth = inputs.shape[0] + 3 * rank
    height = HEIGHT

    def fixed(shape):
        return pl.BlockSpec(shape, lambda step: (0, 0))

    block = pl.BlockSpec((1, height, columns), lambda step: (0, step, 0))
    return pl.pallas_call(
        functools.partial(residual_kernel, math.sqrt(rows * pairs)),
        name="residual",
        grid=(rows // height,),
        out_shape=(
            jax.ShapeDtypeStruct(error.shape, jnp.bfloat16),
            jax.ShapeDtypeStruct((rank, rows), jnp.bfloat16),
            jax.ShapeDtypeStruct((rank, columns), jnp.bfloat16),
        ),
        in_specs=[fixed(v.shape) for v in (inputs, out_grads, q3, basis)] + [block],
        out_specs=[block, fixed((rank, rows)), fixed((rank, columns))],
        scratch_shapes=[
            pltpu.VMEM((depth, rows), jnp.bfloat16),
            pltpu.VMEM((depth, columns), jnp.bfloat16),
        ],
        compiler_params=pltpu.CompilerParams(vmem_limit_bytes=40 << 20),
    )(inputs, out_grads, q3, basis, error)


def rounded_pieces(value):
    pieces = []
    for _ in range(PIECES):
        piece = lax.reduce_precision(value, 8, 7)
        pieces.append(piece.astype(jnp.bfloat16))
        value = value - piece
    return jnp.concatenate(pieces, axis=0)


def plain_left(replicas, rank, a, q3, inputs, out_grads):
    inner = fold(contract(q3, out_grads, 1, 1), rank)
    outer = fold(contract(rounded_pieces(inner), inputs, 1, 0), rank)
    p = lax.psum((outer + fold(a, rank)) / replicas, ("rep", "fsdp"))
    return p, rounded_pieces(p)


def plain_right(replicas, rank, a, p, p3, inputs, out_grads):
    inner = fold(contract(p3, inputs, 1, 1), rank)
    outer = fold(contract(rounded_pieces(inner), out_grads, 1, 0), rank)
    q = lax.psum((outer + fold(a, rank)) / replicas, ("rep", "tp"))
    gram = lax.psum(contract(p, p, 1, 1, exact_mode), "tp")
    inverse = jax.scipy.linalg.solve_triangular(
        jnp.linalg.cholesky(gram), jnp.eye(rank, dtype=jnp.float32), lower=True
    )
    q = contract(inverse, q, 1, 0, exact_mode)
    return q, rounded_pieces(q), contract(inverse, p, 1, 0, exact_mode)


def shards(inputs, out_grads, error, q_init):
    replicas, splits, pairs = lax.axis_size("rep"), lax.axis_size("fsdp"), lax.axis_size("tp")
    rank = q_init.shape[1]
    rows, columns = error.shape[1:]
    left_group = Group("fsdp", replicas, splits)
    right_group = Group("tp", replicas, pairs)
    if (
        replicas % 2 == 0 and rank == 64 and pairs > 1 and left_group.count > 1
        and rows % (left_group.count * 128) == 0 and rows % HEIGHT == 0
        and rank % (right_group.count * 16) == 0 and columns % BLOCK == 0
    ):
        q3, basis = factor_call(
            left_group, right_group, pairs, replicas, rank, q_init.T, inputs, out_grads, error
        )
        new_error, p_factor, q_factor = residual_call(
            pairs, q3, basis, inputs, out_grads, error
        )
        return (new_error, p_factor.T, q_factor.T)
    q3 = q_init.T
    for _ in range(ITERS):
        a = contract(q3, error[0], 1, 1)
        p, p3 = plain_left(replicas, rank, a, q3, inputs, out_grads)
        a = contract(p3, error[0], 1, 0)
        q, q3, basis = plain_right(replicas, rank, a, p, p3, inputs, out_grads)
    basis3 = rounded_pieces(-basis)
    high, low = basis3[:rank], basis3[rank : 2 * rank]
    lefts = jnp.concatenate([inputs, high, high, low], axis=0)
    rights = jnp.concatenate([out_grads, q3[:rank], q3[rank : 2 * rank], q3[:rank]], axis=0)
    merged = contract(lefts, rights, 0, 0) + error[0].astype(jnp.float32)
    p_factor = (basis * math.sqrt(rows * pairs)).astype(jnp.bfloat16).T
    return (merged.astype(jnp.bfloat16)[None], p_factor, q.astype(jnp.bfloat16).T)


def solution(mesh):
    in_specs = (P("rep", "tp"), P("rep", "fsdp"), P("rep", "tp", "fsdp"), P("fsdp", None))
    out_specs = (P("rep", "tp", "fsdp"), P("tp", None), P("fsdp", None))
    return jax.shard_map(shards, mesh=mesh, in_specs=in_specs, out_specs=out_specs, check_vma=False)
```
